32 devices in a mesh: band: 16 (over z, x, core), ga: 2 (over y).
Axes of the slice: x: 2, y: 2, z: 4, core: 2. Of those that a mesh axis runs over, the one named last changes fastest.
Arguments:
- psi: float32 [8192, 8192], P('ga', 'band'), may hold values from -6 to 6
- tiles: float32 [16, 3, 512, 512], P('band', None, 'ga'), may hold values from -0.1875 to 0.1875
- half_width: int32 [1], replicated, may hold values from 384 to 512
Outputs:
- rotated: float32 [8192, 8192], P('ga', 'band')
The draws below stay inside these ranges and needn't reach their ends.
All inputs are finite; a program needn't handle non-finite values.
Results may differ from the reference program's by a relative error of at most 0.0001.
Values sent between devices are 32-bit elements; how exact they have to be, the bound alone decides.
A program may use at most 128 MiB of HBM per device.

```python
import jax
import jax.numpy as jnp
from jax import lax

NB = 8192
HALF = 512
BB = 512
REACH = 1
GV = 8192
N_BAND = 16


def block_scale(key, shape, split, smallest, top_value):
    level = 1.0
    for axis_at, parts in split:
        steps = jax.random.uniform(jax.random.fold_in(jax.random.fold_in(key, 6), axis_at), (parts,), jnp.float32, smallest / len(split), top_value / len(split))
        level = level * jnp.repeat(jnp.exp(steps), shape[axis_at] // parts).reshape((-1,) + (1,) * (len(shape) - 1 - axis_at))
    return level


def gaussian(own_key, dims, scale, most, cuts=(), held_as=jnp.bfloat16):
    array = scale * jax.random.normal(own_key, dims, jnp.float32)
    if cuts:
        array = array * block_scale(own_key, dims, cuts, -0.22, 0.18)
    return jnp.clip(array, -most, most).astype(held_as)


def setup_inputs(seed: int = 0) -> dict:
    key_list = jax.random.split(jax.random.key(seed), 4)
    return {
        "psi": gaussian(key_list[0], (GV, NB), 1.0, 6.0, ((0, 2), (1, 16)), jnp.float32),
        "tiles": gaussian(key_list[1], (N_BAND, 2 * REACH + 1, BB, BB), (2 * HALF) ** -0.5, 0.1875, ((0, 16), (2, 2)), jnp.float32),
        "half_width": jax.random.randint(key_list[2], (1,), HALF * 3 // 4, HALF + 1).astype(jnp.int32),
    }


def band_mask(span, width, half_width):
    reach = (span - 1) // 2
    index = jnp.arange(width).astype(jnp.int32)
    shifts = (jnp.arange(span).astype(jnp.int32) - reach) * width
    offsets = shifts[:, None, None] + index[None, :, None] - index[None, None, :]
    return (jnp.abs(offsets) <= half_width[0]).astype(jnp.float32)


def reference(psi, tiles, half_width):
    rows = psi.shape[0]
    blocks_count, span, width = tiles.shape[0], tiles.shape[1], tiles.shape[2]
    reach = (span - 1) // 2
    masked = tiles * band_mask(span, width, half_width)[None]
    blocks = psi.reshape(rows, blocks_count, width)
    padded = jnp.pad(blocks, ((0, 0), (reach, reach), (0, 0)))
    result = jnp.zeros((rows, blocks_count, width), jnp.float32)
    for k in range(span):
        panel = padded[:, k:k + blocks_count, :]
        result = result + jnp.einsum("gjb,jbc->gjc", panel, masked[:, k], precision=lax.Precision.HIGHEST)
    return result.reshape(rows, blocks_count * width)
```

```python
import functools
import math

import jax
import jax.numpy as jnp
from jax import lax
from jax.experimental import pallas as pl
from jax.experimental.pallas import tpu as pltpu
from jax.sharding import PartitionSpec as P

MESH = pl.DeviceIdType.MESH
CHUNKS = 16
FIRST = 4
LANES = 128
SUB = 256
LEVELS = 16
AHEAD = 2


def split(x):
    high = x.astype(jnp.bfloat16)
    return high, (x - high.astype(jnp.float32)).astype(jnp.bfloat16)


def product(x, high, low):
    x_high, x_low = split(x)
    dot = functools.partial(jnp.dot, preferred_element_type=jnp.float32)
    return dot(x_high, high) + (dot(x_high, low) + dot(x_low, high))


def kernel(n, n_ga, plane, edge, hw_ref, psi, tiles, out, own, near, relay, raw, high, low,
           edge_own, edge_near, edge_relay, own_sem, tile_send, tile_recv, send, recv, relay_recv,
           forward_send, edge_send, edge_recv, edge_relay_recv, edge_forward_send):
    me = lax.axis_index("band")
    ga = lax.axis_index("ga")
    rows, width = psi.shape
    span, part = tiles.shape[1], tiles.shape[2]
    reach = (span - 1) // 2
    chunk = rows // CHUNKS
    sub = math.gcd(chunk, SUB)
    edge_at = (LANES - edge, 0)
    planes = n // plane
    relays = plane >= 4 and planes > 1
    moves = [s * m for m in range(1, reach + 1) for s in (1, -1)]
    at, last = lax.rem(me, plane), lax.div(me, plane)

    peers = []
    for move in moves:
        there = me + move
        peers.append(((there >= 0) & (there < n), there))
        back = me - move
        peers.append(((back >= 0) & (back < n), back))
    up_src = (at == plane - 1) & (last < planes - 1)
    up_mid = (at == 0) & (last < planes - 1)
    up_dst = (at == 0) & (last > 0)
    down_src = (at == 0) & (last > 0)
    down_mid = (at == plane - 2) & (last > 0)
    down_dst = (at == plane - 1) & (last < planes - 1)
    up_mid_of_src = me - (plane - 1)
    down_mid_of_src = me + (plane - 2)
    if relays:
        peers += [
            (up_src, me - (plane - 1)), (up_mid, me + (plane - 1)),
            (up_mid, me + plane), (up_dst, me - plane),
            (down_src, me + (plane - 2)), (down_mid, me - (plane - 2)),
            (down_mid, me - (plane - 1)), (down_dst, me + (plane - 1)),
        ]
    barrier = pltpu.get_barrier_semaphore()
    count = jnp.int32(n_ga - 1)
    for step in range(1, n_ga):
        pl.semaphore_signal(barrier, inc=1, device_id=(me, lax.rem(ga + step, n_ga)), device_id_type=MESH)
    for cond, peer in peers:
        @pl.when(cond)
        def _(peer=peer):
            pl.semaphore_signal(barrier, inc=1, device_id=(peer, ga), device_id_type=MESH)
        count = count + cond.astype(jnp.int32)
    pl.semaphore_wait(barrier, count)

    def block(c):
        return pl.ds(pl.multiple_of(c * chunk, chunk), chunk)

    def columns(slot, move):
        if abs(move) != reach:
            return pl.ds(0, width)
        return pl.ds(LANES if slot % 2 == 0 else 0, width - LANES)

    def direct_copy(slot, move, c):
        at_ = (block(c), columns(slot, move))
        return pltpu.make_async_remote_copy(
            psi.at[at_], near.at[(slot, *at_)], send.at[slot, c], recv.at[slot, c],
            device_id=(me + move, ga), device_id_type=MESH)

    def relay_copy(slot, mid, c):
        at_ = (block(c), columns(slot, moves[slot]))
        return pltpu.make_async_remote_copy(
            psi.at[at_], relay.at[at_], send.at[slot, c], relay_recv.at[c],
            device_id=(mid, ga), device_id_type=MESH)

    def forward_copy(slot, to, c):
        at_ = (block(c), columns(slot, moves[slot]))
        return pltpu.make_async_remote_copy(
            relay.at[at_], near.at[(slot, *at_)], forward_send.at[c], recv.at[slot, c],
            device_id=(to, ga), device_id_type=MESH)

    def edge_direct(side, move, c):
        at_ = pl.ds(edge_at[side], edge)
        return pltpu.make_async_remote_copy(
            edge_own.at[side, c, at_], edge_near.at[side, c, at_],
            edge_send.at[side, c], edge_recv.at[side, c],
            device_id=(me + move, ga), device_id_type=MESH)

    def edge_relayed(side, mid, c):
        at_ = pl.ds(edge_at[side], edge)
        return pltpu.make_async_remote_copy(
            edge_own.at[side, c, at_], edge_relay.at[c, at_],
            edge_send.at[side, c], edge_relay_recv.at[c],
            device_id=(mid, ga), device_id_type=MESH)

    def edge_forward(side, to, c):
        at_ = pl.ds(edge_at[side], edge)
        return pltpu.make_async_remote_copy(
            edge_relay.at[c, at_], edge_near.at[side, c, at_],
            edge_forward_send.at[c], edge_recv.at[side, c],
            device_id=(to, ga), device_id_type=MESH)

    def goes_up(p, c):
        return lax.rem(c, planes) < planes - 1 - p

    def goes_down(p, c):
        return lax.rem(c, planes) < p

    def tile_copy(step):
        peer = lax.rem(ga + step, n_ga)
        return pltpu.make_async_remote_copy(
            tiles.at[0], raw.at[:, pl.ds(pl.multiple_of(ga * part, part), part), :],
            tile_send.at[step - 1], tile_recv.at[step - 1],
            device_id=(me, peer), device_id_type=MESH)

    def send_from(slot, move, c, straight, through):
        there = me + move
        valid = (there >= 0) & (there < n)
        if relays and abs(move) == 1:
            src, mid = (up_src, up_mid_of_src) if move == 1 else (down_src, down_mid_of_src)
            via = src & (goes_up(last, c) if move == 1 else goes_down(last, c))

            @pl.when(via)
            def _():
                through(slot, mid, c).start()
            valid = valid & jnp.logical_not(via)

        @pl.when(valid)
        def _():
            straight(slot, move, c).start()

    def start(c):
        for slot, move in enumerate(moves):
            send_from(slot, move, c, direct_copy, relay_copy)

    def start_first(c, carry):
        start(c)
        return carry
    lax.fori_loop(0, FIRST, start_first, 0)
    for step in range(1, n_ga):
        tile_copy(step).start()

    own_psi = pltpu.make_async_copy(psi, own, own_sem.at[0])
    own_psi.start()
    own_tiles = pltpu.make_async_copy(
        tiles.at[0], raw.at[:, pl.ds(pl.multiple_of(ga * part, part), part), :], own_sem.at[1])
    own_tiles.start()
    own_psi.wait()
    outer = (reach, -reach)

    def within(first, i, size):
        return pl.ds(pl.multiple_of(first + i * size, size), size)

    def start_rest(c, carry):
        rows_ = block(c)
        edge_own[0, c] = jnp.transpose(own[rows_, 0:LANES])
        edge_own[1, c] = jnp.transpose(own[rows_, width - LANES:width])
        for side, move in enumerate(outer):
            send_from(side, move, c, edge_direct, edge_relayed)

        @pl.when(c + FIRST < CHUNKS)
        def _():
            start(c + FIRST)
        return carry
    lax.fori_loop(0, CHUNKS, start_rest, 0)

    if edge < LANES:
        def clear(c, carry):
            blank = jnp.zeros((LANES - edge, chunk), jnp.float32)
            edge_near[0, c, 0:LANES - edge, :] = blank
            edge_near[1, c, edge:LANES, :] = blank
            return carry
        lax.fori_loop(0, CHUNKS, clear, 0)

    own_tiles.wait()
    for step in range(1, n_ga):
        tile_copy(step).wait_recv()
    half = hw_ref[0]
    piece = min(width, 128)
    pieces = width // piece

    def mask(i, carry):
        k, r = lax.div(i, pieces), lax.rem(i, pieces) * piece
        at_ = pl.ds(pl.multiple_of(r, piece), piece)
        row = lax.broadcasted_iota(jnp.int32, (piece, width), 0) + (r + (k - reach) * width)
        col = lax.broadcasted_iota(jnp.int32, (piece, width), 1)
        u = jnp.where(jnp.abs(row - col) <= half, raw[k, at_, :], 0.0)
        high[k, at_, :], low[k, at_, :] = split(u)
        return carry
    lax.fori_loop(0, span * pieces, mask, 0)
    def centre(c, carry):
        at_ = within(0, c, sub)
        out[at_, :] = product(own[at_, :], high[reach], low[reach])
        return carry
    lax.fori_loop(0, rows // sub, centre, 0)

    def pass_on(c, arrive, forward):
        @pl.when(up_mid & goes_up(last, c))
        def _():
            arrive(0, me, c).wait_recv()
            forward(0, me + plane, c).start()

        @pl.when(down_mid & goes_down(last, c))
        def _():
            arrive(1, me, c).wait_recv()
            forward(1, me - (plane - 1), c).start()

    def relay_on(c):
        pass_on(c, relay_copy, forward_copy)
        if reach == 1:
            pass_on(c, edge_relayed, edge_forward)

    def add(slot, move, c):
        direct_copy(slot, move, c).wait_recv()
        k = reach - move
        cols = columns(slot, move)
        x = near[slot, block(c), cols.start:cols.start + cols.size]
        if abs(move) == reach:
            side = slot % 2
            edge_direct(side, move, c).wait_recv()
            turned = jnp.transpose(edge_near[side, c])
            x = jnp.concatenate([turned, x] if side == 0 else [x, turned], axis=1)
        out[block(c), :] += product(x, high[k], low[k])

    def sides_of(turn, carry):
        def step(c, inner):
            if relays:
                @pl.when((turn == 1) & (c + AHEAD < CHUNKS))
                def _():
                    relay_on(c + AHEAD)
            for slot, move in enumerate(moves):
                back = me - move
                here = (abs(move) == 1) & (lax.rem(me, 2) == (1 if move == 1 else 0))

                @pl.when((back >= 0) & (back < n) & (here == (turn == 0)))
                def _(slot=slot, move=move):
                    add(slot, move, c)
            return inner
        lax.fori_loop(0, CHUNKS, step, 0)
        if relays:
            @pl.when(turn == 0)
            def _():
                for c in range(AHEAD):
                    relay_on(jnp.int32(c))
        return carry
    lax.fori_loop(0, 2, sides_of, 0)

    def finish(c, carry):
        for slot, move in enumerate(moves):
            there = me + move

            @pl.when((there >= 0) & (there < n))
            def _():
                direct_copy(slot, move, c).wait_send()
        if relays:
            @pl.when((up_mid & goes_up(last, c)) | (down_mid & goes_down(last, c)))
            def _():
                forward_copy(0, me, c).wait_send()
        return carry
    lax.fori_loop(0, CHUNKS, finish, 0)

    def edge_finish(c, carry):
        for side, move in enumerate(outer):
            there = me + move

            @pl.when((there >= 0) & (there < n))
            def _():
                edge_direct(side, move, c).wait_send()
        if relays and reach == 1:
            @pl.when((up_mid & goes_up(last, c)) | (down_mid & goes_down(last, c)))
            def _():
                edge_forward(0, me, c).wait_send()
        return carry
    lax.fori_loop(0, CHUNKS, edge_finish, 0)
    for step_ in range(1, n_ga):
        tile_copy(step_).wait_send()


def plane_size(mesh):
    axis = mesh.axis_names.index("band")
    line = mesh.devices.take(0, axis=1 - axis)
    coords = [getattr(d, "coords", None) for d in line]
    if coords[0] is None:
        return len(coords)
    return sum(c[2] == coords[0][2] for c in coords)


def solution(mesh):
    n, n_ga = mesh.shape["band"], mesh.shape["ga"]
    plane = plane_size(mesh)

    def rotate(level, psi, tiles, half_width):
        rows, width = psi.shape
        span = tiles.shape[1]
        sides = span - 1
        edge = LANES * (level + 1) // LEVELS
        f32, bf16 = jnp.float32, jnp.bfloat16
        dma = pltpu.SemaphoreType.DMA
        edge_shape = (CHUNKS, LANES, rows // CHUNKS)
        return pl.pallas_call(
            functools.partial(kernel, n, n_ga, plane, edge),
            out_shape=pltpu.VMEM((rows, width), f32),
            in_specs=[
                pl.BlockSpec(memory_space=pltpu.SMEM),
                pl.BlockSpec(memory_space=pl.ANY),
                pl.BlockSpec(memory_space=pl.ANY),
            ],
            out_specs=pl.BlockSpec(memory_space=pltpu.VMEM),
            scratch_shapes=[
                pltpu.VMEM((rows, width), f32),
                pltpu.VMEM((sides, rows, width), f32),
                pltpu.VMEM((rows, width), f32),
                pltpu.VMEM((span, width, width), f32),
                pltpu.VMEM((span, width, width), bf16),
                pltpu.VMEM((span, width, width), bf16),
                pltpu.VMEM((2, *edge_shape), f32),
                pltpu.VMEM((2, *edge_shape), f32),
                pltpu.VMEM(edge_shape, f32),
                dma((2,)),
                dma((n_ga - 1,)),
                dma((n_ga - 1,)),
                dma((sides, CHUNKS)),
                dma((sides, CHUNKS)),
                dma((CHUNKS,)),
                dma((CHUNKS,)),
                dma((2, CHUNKS)),
                dma((2, CHUNKS)),
                dma((CHUNKS,)),
                dma((CHUNKS,)),
            ],
            compiler_params=pltpu.CompilerParams(
                collective_id=level, has_side_effects=True, vmem_limit_bytes=52 * 2**20),
            name=f"rotate_{edge}",
        )(half_width, psi, tiles)

    def on_device(psi, tiles, half_width):
        width = psi.shape[1]
        reach = (tiles.shape[1] - 1) // 2
        beyond = half_width[0] - (reach * width - LANES + 1)
        level = lax.shift_right_arithmetic(beyond, (LANES // LEVELS).bit_length() - 1)
        branches = [functools.partial(rotate, i) for i in range(LEVELS)]
        return lax.switch(level, branches, psi, tiles, half_width)

    return jax.shard_map(
        on_device,
        mesh=mesh,
        in_specs=(P("ga", "band"), P("band", None, "ga", None), P()),
        out_specs=P("ga", "band"),
        check_vma=False,
    )
```

```python
import functools
import math

import jax
import jax.numpy as jnp
from jax import lax
from jax.experimental import pallas as pl
from jax.experimental.pallas import tpu as pltpu
from jax.sharding import PartitionSpec as P

MESH = pl.DeviceIdType.MESH
CHUNKS = 16
FIRST = 4
LANES = 128
SUB = 256
LEVELS = 16
AHEAD = 2


def split(x):
    high = x.astype(jnp.bfloat16)
    return high, (x - high.astype(jnp.float32)).astype(jnp.bfloat16)


def product(x, high, low):
    x_high, x_low = split(x)
    dot = functools.partial(jnp.dot, preferred_element_type=jnp.float32)
    return dot(x_high, high) + (dot(x_high, low) + dot(x_low, high))


def kernel(n, n_ga, plane, edge, half_width, psi, tiles, out, held, own, near, relay, raw, high, low,
           edge_own, edge_near, edge_relay, own_sem, tile_send, tile_recv, send, recv, relay_recv,
           forward_send, edge_send, edge_recv, edge_relay_recv, edge_forward_send):
    me = lax.axis_index("band")
    ga = lax.axis_index("ga")
    rows, width = psi.shape
    span, part = tiles.shape[1], tiles.shape[2]
    reach = (span - 1) // 2
    chunk = rows // CHUNKS
    sub = math.gcd(chunk, SUB)
    edge_at = (LANES - edge, 0)
    planes = n // plane
    relays = plane >= 4 and planes > 1
    moves = [s * m for m in range(1, reach + 1) for s in (1, -1)]
    at, last = lax.rem(me, plane), lax.div(me, plane)

    peers = []
    for move in moves:
        there = me + move
        peers.append(((there >= 0) & (there < n), there))
    up_src = (at == plane - 1) & (last < planes - 1)
    up_mid = (at == 0) & (last < planes - 1)
    up_dst = (at == 0) & (last > 0)
    down_src = (at == 0) & (last > 0)
    down_mid = (at == plane - 1) & (last > 0)
    down_dst = (at == plane - 1) & (last < planes - 1)
    up_mid_of_src = me - (plane - 1)
    down_mid_of_src = me + (plane - 1)
    if relays:
        peers += [
            (up_src, me - (plane - 1)), (up_mid, me + (plane - 1)),
            (up_mid, me + plane), (up_dst, me - plane),
            (down_src, me + (plane - 1)), (down_mid, me - (plane - 1)),
            (down_mid, me - plane), (down_dst, me + plane),
        ]
    barrier = pltpu.get_barrier_semaphore()
    count = jnp.int32(n_ga - 1)
    for step in range(1, n_ga):
        pl.semaphore_signal(barrier, inc=1, device_id=(me, lax.rem(ga + step, n_ga)), device_id_type=MESH)
    for cond, peer in peers:
        @pl.when(cond)
        def _(peer=peer):
            pl.semaphore_signal(barrier, inc=1, device_id=(peer, ga), device_id_type=MESH)
        count = count + cond.astype(jnp.int32)
    pl.semaphore_wait(barrier, count)

    def block(c):
        return pl.ds(pl.multiple_of(c * chunk, chunk), chunk)

    def columns(slot, move):
        if abs(move) != reach:
            return pl.ds(0, width)
        return pl.ds(LANES if slot % 2 == 0 else 0, width - LANES)

    def direct_copy(slot, move, c):
        at_ = (block(c), columns(slot, move))
        return pltpu.make_async_remote_copy(
            psi.at[at_], near.at[(slot, *at_)], send.at[slot], recv.at[slot, c],
            device_id=(me + move, ga), device_id_type=MESH)

    def relay_copy(slot, mid, c):
        at_ = (block(c), columns(slot, moves[slot]))
        return pltpu.make_async_remote_copy(
            psi.at[at_], relay.at[at_], send.at[slot], relay_recv.at[c],
            device_id=(mid, ga), device_id_type=MESH)

    def forward_copy(slot, to, c):
        at_ = (block(c), columns(slot, moves[slot]))
        return pltpu.make_async_remote_copy(
            relay.at[at_], near.at[(slot, *at_)], forward_send.at[c], recv.at[slot, c],
            device_id=(to, ga), device_id_type=MESH)

    def edge_direct(side, move, c):
        at_ = pl.ds(edge_at[side], edge)
        return pltpu.make_async_remote_copy(
            edge_own.at[side, c, at_], edge_near.at[side, c, at_],
            edge_send.at[side], edge_recv.at[side, c],
            device_id=(me + move, ga), device_id_type=MESH)

    def edge_relayed(side, mid, c):
        at_ = pl.ds(edge_at[side], edge)
        return pltpu.make_async_remote_copy(
            edge_own.at[side, c, at_], edge_relay.at[c, at_],
            edge_send.at[side], edge_relay_recv.at[c],
            device_id=(mid, ga), device_id_type=MESH)

    def edge_forward(side, to, c):
        at_ = pl.ds(edge_at[side], edge)
        return pltpu.make_async_remote_copy(
            edge_relay.at[c, at_], edge_near.at[side, c, at_],
            edge_forward_send.at[c], edge_recv.at[side, c],
            device_id=(to, ga), device_id_type=MESH)

    def goes_up(p, c):
        return lax.rem(c, planes) < planes - 1 - p

    def goes_down(p, c):
        return lax.rem(c, planes) < p

    def tile_copy(step):
        peer = lax.rem(ga + step, n_ga)
        return pltpu.make_async_remote_copy(
            tiles.at[0], raw.at[:, pl.ds(pl.multiple_of(ga * part, part), part), :],
            tile_send.at[step - 1], tile_recv.at[step - 1],
            device_id=(me, peer), device_id_type=MESH)

    def send_from(slot, move, c, straight, through):
        there = me + move
        valid = (there >= 0) & (there < n)
        if relays and abs(move) == 1:
            src, mid = (up_src, up_mid_of_src) if move == 1 else (down_src, down_mid_of_src)
            via = src & (goes_up(last, c) if move == 1 else goes_down(last, c))

            @pl.when(via)
            def _():
                through(slot, mid, c).start()
            valid = valid & jnp.logical_not(via)

        @pl.when(valid)
        def _():
            straight(slot, move, c).start()

    def start(c, carry):
        for slot, move in enumerate(moves):
            send_from(slot, move, c, direct_copy, relay_copy)
        return carry

    lax.fori_loop(0, FIRST, start, 0)
    for step in range(1, n_ga):
        tile_copy(step).start()

    own_psi = pltpu.make_async_copy(psi, own, own_sem.at[0])
    own_psi.start()
    own_tiles = pltpu.make_async_copy(
        tiles.at[0], raw.at[:, pl.ds(pl.multiple_of(ga * part, part), part), :], own_sem.at[1])
    own_tiles.start()
    own_half = pltpu.make_async_copy(half_width, held, own_sem.at[2])
    own_half.start()
    own_psi.wait()
    outer = (reach, -reach)

    def within(first, i, size):
        return pl.ds(pl.multiple_of(first + i * size, size), size)

    def start_edge(c, carry):
        rows_ = block(c)
        edge_own[0, c] = jnp.transpose(own[rows_, 0:LANES])
        edge_own[1, c] = jnp.transpose(own[rows_, width - LANES:width])
        for side, move in enumerate(outer):
            send_from(side, move, c, edge_direct, edge_relayed)
        return carry
    lax.fori_loop(0, CHUNKS, start_edge, 0)
    lax.fori_loop(FIRST, CHUNKS, start, 0)

    if edge < LANES:
        def clear(c, carry):
            blank = jnp.zeros((LANES - edge, chunk), jnp.float32)
            edge_near[0, c, 0:LANES - edge, :] = blank
            edge_near[1, c, edge:LANES, :] = blank
            return carry
        lax.fori_loop(0, CHUNKS, clear, 0)

    own_tiles.wait()
    for step in range(1, n_ga):
        tile_copy(step).wait_recv()
    own_half.wait()
    half = held[0]
    piece = min(width, 128)
    pieces = width // piece

    def mask(i, carry):
        k, r = lax.div(i, pieces), lax.rem(i, pieces) * piece
        at_ = pl.ds(pl.multiple_of(r, piece), piece)
        row = lax.broadcasted_iota(jnp.int32, (piece, width), 0) + (r + (k - reach) * width)
        col = lax.broadcasted_iota(jnp.int32, (piece, width), 1)
        u = jnp.where(jnp.abs(row - col) <= half, raw[k, at_, :], 0.0)
        high[k, at_, :], low[k, at_, :] = split(u)
        return carry
    lax.fori_loop(0, span * pieces, mask, 0)
    def centre(c, carry):
        at_ = within(0, c, sub)
        out[at_, :] = product(own[at_, :], high[reach], low[reach])
        return carry
    lax.fori_loop(0, rows // sub, centre, 0)

    def pass_on(c, arrive, forward):
        @pl.when(up_mid & goes_up(last, c))
        def _():
            arrive(0, me, c).wait_recv()
            forward(0, me + plane, c).start()

        @pl.when(down_mid & goes_down(last, c))
        def _():
            arrive(1, me, c).wait_recv()
            forward(1, me - plane, c).start()

    def relay_on(c):
        pass_on(c, relay_copy, forward_copy)
        if reach == 1:
            pass_on(c, edge_relayed, edge_forward)

    def add(slot, move, c):
        direct_copy(slot, move, c).wait_recv()
        k = reach - move
        cols = columns(slot, move)
        x = near[slot, block(c), cols.start:cols.start + cols.size]
        if abs(move) == reach:
            side = slot % 2
            edge_direct(side, move, c).wait_recv()
            turned = jnp.transpose(edge_near[side, c])
            x = jnp.concatenate([turned, x] if side == 0 else [x, turned], axis=1)
        out[block(c), :] += product(x, high[k], low[k])

    def sides_of(turn, carry):
        def step(c, inner):
            if relays:
                @pl.when((turn == 1) & (c + AHEAD < CHUNKS))
                def _():
                    relay_on(c + AHEAD)
            for slot, move in enumerate(moves):
                back = me - move
                here = (abs(move) == 1) & (lax.rem(me, 2) == (1 if move == 1 else 0))

                @pl.when((back >= 0) & (back < n) & (here == (turn == 0)))
                def _(slot=slot, move=move):
                    add(slot, move, c)
            return inner
        lax.fori_loop(0, CHUNKS, step, 0)
        if relays:
            @pl.when(turn == 0)
            def _():
                for c in range(AHEAD):
                    relay_on(jnp.int32(c))
        return carry
    lax.fori_loop(0, 2, sides_of, 0)

    for slot, move in enumerate(moves):
        there = me + move

        @pl.when((there >= 0) & (there < n))
        def _(slot=slot, move=move):
            all_ = (pl.ds(0, rows), columns(slot, move))
            pltpu.make_async_remote_copy(
                psi.at[all_], near.at[(slot, *all_)], send.at[slot], recv.at[slot, 0],
                device_id=(me + move, ga), device_id_type=MESH).wait_send()
            if abs(move) == reach:
                side = slot % 2
                all_ = (side, pl.ds(0, CHUNKS), pl.ds(edge_at[side], edge))
                pltpu.make_async_remote_copy(
                    edge_own.at[all_], edge_near.at[all_], edge_send.at[side], edge_recv.at[side, 0],
                    device_id=(me + move, ga), device_id_type=MESH).wait_send()

    def finish(c, carry):
        @pl.when((up_mid & goes_up(last, c)) | (down_mid & goes_down(last, c)))
        def _():
            forward_copy(0, me, c).wait_send()
            if reach == 1:
                edge_forward(0, me, c).wait_send()
        return carry
    if relays:
        lax.fori_loop(0, CHUNKS, finish, 0)
    for step_ in range(1, n_ga):
        tile_copy(step_).wait_send()


def plane_size(mesh):
    axis = mesh.axis_names.index("band")
    line = mesh.devices.take(0, axis=1 - axis)
    coords = [getattr(d, "coords", None) for d in line]
    if coords[0] is None:
        return len(coords)
    return sum(c[2] == coords[0][2] for c in coords)


def solution(mesh):
    n, n_ga = mesh.shape["band"], mesh.shape["ga"]
    plane = plane_size(mesh)

    def rotate(level, psi, tiles, half_width):
        rows, width = psi.shape
        span = tiles.shape[1]
        sides = span - 1
        edge = LANES * (level + 1) // LEVELS
        f32, bf16 = jnp.float32, jnp.bfloat16
        dma = pltpu.SemaphoreType.DMA
        edge_shape = (CHUNKS, LANES, rows // CHUNKS)
        return pl.pallas_call(
            functools.partial(kernel, n, n_ga, plane, edge),
            out_shape=pltpu.VMEM((rows, width), f32),
            in_specs=[
                pl.BlockSpec(memory_space=pl.ANY),
                pl.BlockSpec(memory_space=pl.ANY),
                pl.BlockSpec(memory_space=pl.ANY),
            ],
            out_specs=pl.BlockSpec(memory_space=pltpu.VMEM),
            scratch_shapes=[
                pltpu.SMEM((1,), jnp.int32),
                pltpu.VMEM((rows, width), f32),
                pltpu.VMEM((sides, rows, width), f32),
                pltpu.VMEM((rows, width), f32),
                pltpu.VMEM((span, width, width), f32),
                pltpu.VMEM((span, width, width), bf16),
                pltpu.VMEM((span, width, width), bf16),
                pltpu.VMEM((2, *edge_shape), f32),
                pltpu.VMEM((2, *edge_shape), f32),
                pltpu.VMEM(edge_shape, f32),
                dma((3,)),
                dma((n_ga - 1,)),
                dma((n_ga - 1,)),
                dma((sides,)),
                dma((sides, CHUNKS)),
                dma((CHUNKS,)),
                dma((CHUNKS,)),
                dma((2,)),
                dma((2, CHUNKS)),
                dma((CHUNKS,)),
                dma((CHUNKS,)),
            ],
            compiler_params=pltpu.CompilerParams(
                collective_id=level, has_side_effects=True, vmem_limit_bytes=52 * 2**20),
            name=f"rotate_{edge}",
        )(half_width, psi, tiles)

    def on_device(psi, tiles, half_width):
        width = psi.shape[1]
        reach = (tiles.shape[1] - 1) // 2
        beyond = half_width[0] - (reach * width - LANES + 1)
        level = lax.shift_right_arithmetic(beyond, (LANES // LEVELS).bit_length() - 1)
        branches = [functools.partial(rotate, i) for i in range(LEVELS)]
        return lax.switch(level, branches, psi, tiles, half_width)

    return jax.shard_map(
        on_device,
        mesh=mesh,
        in_specs=(P("ga", "band"), P("band", None, "ga", None), P()),
        out_specs=P("ga", "band"),
        check_vma=False,
    )
```

```python
import functools

import jax
import jax.numpy as jnp
from jax import lax
from jax.experimental import pallas as pl
from jax.experimental.pallas import tpu as pltpu
from jax.sharding import PartitionSpec as P

MESH = pl.DeviceIdType.MESH
CHUNKS = 16
FIRST = 4
EDGES = 4
LANES = 128
LEVELS = 16
AHEAD = 2


def split(x):
    high = x.astype(jnp.bfloat16)
    return high, (x - high.astype(jnp.float32)).astype(jnp.bfloat16)


def product(x, high, low):
    x_high, x_low = split(x)
    dot = functools.partial(jnp.dot, preferred_element_type=jnp.float32)
    return dot(x_high, high) + (dot(x_high, low) + dot(x_low, high))


def kernel(n, n_ga, plane, edge, half_width, psi, tiles, out, held, near, relay, raw, high, low,
           edge_own, edge_near, edge_relay, own_sem, tile_send, tile_recv, send, recv, relay_recv,
           forward_send, edge_send, edge_recv, edge_relay_recv):
    me = lax.axis_index("band")
    ga = lax.axis_index("ga")
    rows, width = psi.shape
    span, part = tiles.shape[1], tiles.shape[2]
    reach = (span - 1) // 2
    chunk = rows // CHUNKS
    sides = span - 1
    group = CHUNKS // EDGES
    edge_at = (LANES - edge, 0)
    planes = n // plane
    relays = plane >= 4 and planes > 1
    moves = [s * m for m in range(1, reach + 1) for s in (1, -1)]
    at, last = lax.rem(me, plane), lax.div(me, plane)

    peers = []
    for move in moves:
        there = me + move
        peers.append(((there >= 0) & (there < n), there))
    up_src = (at == plane - 1) & (last < planes - 1)
    up_mid = (at == 0) & (last < planes - 1)
    up_dst = (at == 0) & (last > 0)
    down_src = (at == 0) & (last > 0)
    down_mid = (at == plane - 1) & (last > 0)
    down_dst = (at == plane - 1) & (last < planes - 1)
    up_mid_of_src = me - (plane - 1)
    down_mid_of_src = me + (plane - 1)
    if relays:
        peers += [
            (up_src, me - (plane - 1)), (up_mid, me + (plane - 1)),
            (up_mid, me + plane), (up_dst, me - plane),
            (down_src, me + (plane - 1)), (down_mid, me - (plane - 1)),
            (down_mid, me - plane), (down_dst, me + plane),
        ]
    barrier = pltpu.get_barrier_semaphore()
    count = jnp.int32(n_ga - 1)
    for step in range(1, n_ga):
        pl.semaphore_signal(barrier, inc=1, device_id=(me, lax.rem(ga + step, n_ga)), device_id_type=MESH)
    for cond, peer in peers:
        @pl.when(cond)
        def _(peer=peer):
            pl.semaphore_signal(barrier, inc=1, device_id=(peer, ga), device_id_type=MESH)
        count = count + cond.astype(jnp.int32)
    pl.semaphore_wait(barrier, count)

    def block(c):
        return pl.ds(pl.multiple_of(c * chunk, chunk), chunk)

    def columns(slot, move):
        if abs(move) != reach:
            return pl.ds(0, width)
        return pl.ds(LANES if slot % 2 == 0 else 0, width - LANES)

    def direct_copy(slot, move, c):
        at_ = (block(c), columns(slot, move))
        return pltpu.make_async_remote_copy(
            psi.at[at_], near.at[(slot, *at_)], send.at[slot], recv.at[slot, c],
            device_id=(me + move, ga), device_id_type=MESH)

    def relay_copy(slot, mid, c):
        at_ = (block(c), columns(slot, moves[slot]))
        return pltpu.make_async_remote_copy(
            psi.at[at_], relay.at[at_], send.at[slot], relay_recv.at[c],
            device_id=(mid, ga), device_id_type=MESH)

    def forward_copy(slot, to, c):
        at_ = (block(c), columns(slot, moves[slot]))
        return pltpu.make_async_remote_copy(
            relay.at[at_], near.at[(slot, *at_)], forward_send.at[0], recv.at[slot, c],
            device_id=(to, ga), device_id_type=MESH)

    def edge_direct(side, move, c):
        at_ = pl.ds(edge_at[side], edge)
        return pltpu.make_async_remote_copy(
            edge_own.at[side, c, at_], edge_near.at[side, c, at_],
            edge_send.at[side], edge_recv.at[side, c],
            device_id=(me + move, ga), device_id_type=MESH)

    def edge_relayed(side, mid, c):
        at_ = pl.ds(edge_at[side], edge)
        return pltpu.make_async_remote_copy(
            edge_own.at[side, c, at_], edge_relay.at[c, at_],
            edge_send.at[side], edge_relay_recv.at[c],
            device_id=(mid, ga), device_id_type=MESH)

    def edge_forward(side, to, c):
        at_ = pl.ds(edge_at[side], edge)
        return pltpu.make_async_remote_copy(
            edge_relay.at[c, at_], edge_near.at[side, c, at_],
            forward_send.at[1], edge_recv.at[side, c],
            device_id=(to, ga), device_id_type=MESH)

    def goes_up(p, c):
        return lax.rem(c, planes) < planes - 1 - p

    def goes_down(p, c):
        return lax.rem(c, planes) < p

    def tile_copy(step):
        peer = lax.rem(ga + step, n_ga)
        return pltpu.make_async_remote_copy(
            tiles.at[0], raw.at[:, pl.ds(pl.multiple_of(ga * part, part), part), :],
            tile_send.at[step - 1], tile_recv.at[step - 1],
            device_id=(me, peer), device_id_type=MESH)

    def send_from(slot, move, c, straight, through):
        there = me + move
        valid = (there >= 0) & (there < n)
        if relays and abs(move) == 1:
            src, mid = (up_src, up_mid_of_src) if move == 1 else (down_src, down_mid_of_src)
            via = src & (goes_up(last, c) if move == 1 else goes_down(last, c))

            @pl.when(via)
            def _():
                through(slot, mid, c).start()
            valid = valid & jnp.logical_not(via)

        @pl.when(valid)
        def _():
            straight(slot, move, c).start()

    def start(c, carry):
        for slot, move in enumerate(moves):
            send_from(slot, move, c, direct_copy, relay_copy)
        return carry

    lax.fori_loop(0, FIRST, start, 0)
    for step in range(1, n_ga):
        tile_copy(step).start()

    own = near.at[sides]
    own_psi = pltpu.make_async_copy(psi, own, own_sem.at[0])
    own_psi.start()
    own_tiles = pltpu.make_async_copy(
        tiles.at[0], raw.at[:, pl.ds(pl.multiple_of(ga * part, part), part), :], own_sem.at[1])
    own_tiles.start()
    own_half = pltpu.make_async_copy(half_width, held, own_sem.at[2])
    own_half.start()
    own_psi.wait()
    outer = (reach, -reach)

    def lanes_of(c):
        return pl.ds(pl.multiple_of(lax.rem(c, group) * chunk, chunk), chunk)

    def turn_edge(c, carry):
        g = lax.div(c, group)
        edge_own[0, g, :, lanes_of(c)] = jnp.transpose(own[block(c), 0:LANES])
        edge_own[1, g, :, lanes_of(c)] = jnp.transpose(own[block(c), width - LANES:width])

        @pl.when(lax.rem(c, group) == group - 1)
        def _():
            for side, move in enumerate(outer):
                send_from(side, move, g, edge_direct, edge_relayed)
        return carry
    lax.fori_loop(0, CHUNKS, turn_edge, 0)
    lax.fori_loop(FIRST, CHUNKS, start, 0)

    def clear(c, carry):
        out[block(c), :] = jnp.zeros((chunk, width), jnp.float32)
        if edge < LANES:
            blank = jnp.zeros((LANES - edge, chunk), jnp.float32)
            g = lax.div(c, group)
            edge_near[0, g, 0:LANES - edge, lanes_of(c)] = blank
            edge_near[1, g, edge:LANES, lanes_of(c)] = blank
        return carry
    lax.fori_loop(0, CHUNKS, clear, 0)

    own_tiles.wait()
    for step in range(1, n_ga):
        tile_copy(step).wait_recv()
    own_half.wait()
    half = held[0]
    piece = min(width, 128)
    pieces = width // piece

    def mask(i, carry):
        k, r = lax.div(i, pieces), lax.rem(i, pieces) * piece
        at_ = pl.ds(pl.multiple_of(r, piece), piece)
        row = lax.broadcasted_iota(jnp.int32, (piece, width), 0) + (r + (k - reach) * width)
        col = lax.broadcasted_iota(jnp.int32, (piece, width), 1)
        u = jnp.where(jnp.abs(row - col) <= half, raw[k, at_, :], 0.0)
        high[k, at_, :], low[k, at_, :] = split(u)
        return carry
    lax.fori_loop(0, span * pieces, mask, 0)

    def pass_on(c, arrive, forward):
        @pl.when(up_mid & goes_up(last, c))
        def _():
            arrive(0, me, c).wait_recv()
            forward(0, me + plane, c).start()

        @pl.when(down_mid & goes_down(last, c))
        def _():
            arrive(1, me, c).wait_recv()
            forward(1, me - plane, c).start()

    def relay_on(c):
        pass_on(c, relay_copy, forward_copy)
        if reach == 1:
            g = c - (FIRST - 1)

            @pl.when((g >= 0) & (g < EDGES))
            def _():
                pass_on(g, edge_relayed, edge_forward)

    def arrived(slot, move, c):
        if abs(move) == reach:
            side = slot % 2
            g = lax.div(c, group)

            @pl.when(lax.rem(c, group) == 0)
            def _():
                edge_direct(side, move, g).wait_recv()
            lanes = slice(0, LANES) if side == 0 else slice(width - LANES, width)
            near[slot, block(c), lanes] = jnp.transpose(edge_near[side, g, :, lanes_of(c)])
        direct_copy(slot, move, c).wait_recv()

    in_chip = 1 - lax.rem(me, 2)

    def step(i, carry):
        turn, c = lax.div(i, CHUNKS), lax.rem(i, CHUNKS)
        if relays:
            ahead = i - (2 * CHUNKS - AHEAD)

            @pl.when((ahead >= 0) & (ahead < CHUNKS))
            def _():
                relay_on(ahead)

        def add(j, inner):
            other = j + (j >= in_chip).astype(jnp.int32)
            source = jnp.where(turn == 0, sides, jnp.where(turn == 1, in_chip, other))
            far = lax.div(source, 2) + 1
            move = jnp.where(turn == 0, 0, jnp.where(lax.rem(source, 2) == 0, far, -far))
            back = me - move

            @pl.when((back >= 0) & (back < n))
            def _():
                for slot, move_ in enumerate(moves):
                    @pl.when(source == slot)
                    def _(slot=slot, move_=move_):
                        arrived(slot, move_, c)
                k = reach - move
                out[block(c), :] += product(near[source, block(c), :], high[k], low[k])
            return inner
        return lax.fori_loop(0, jnp.where(turn == 2, sides - 1, 1), add, carry)
    lax.fori_loop(0, 3 * CHUNKS, step, 0)

    for slot, move in enumerate(moves):
        there = me + move

        @pl.when((there >= 0) & (there < n))
        def _(slot=slot, move=move):
            all_ = (pl.ds(0, rows), columns(slot, move))
            pltpu.make_async_remote_copy(
                psi.at[all_], near.at[(slot, *all_)], send.at[slot], recv.at[slot, 0],
                device_id=(me + move, ga), device_id_type=MESH).wait_send()
            if abs(move) == reach:
                side = slot % 2
                all_ = (side, pl.ds(0, EDGES), pl.ds(edge_at[side], edge))
                pltpu.make_async_remote_copy(
                    edge_own.at[all_], edge_near.at[all_], edge_send.at[side], edge_recv.at[side, 0],
                    device_id=(me + move, ga), device_id_type=MESH).wait_send()

    def forwarded(slot, steps, edge_steps):
        if steps:
            all_ = (pl.ds(0, steps * chunk), columns(slot, moves[slot]))
            pltpu.make_async_remote_copy(
                relay.at[all_], near.at[(slot, *all_)], forward_send.at[0], recv.at[slot, 0],
                device_id=(me, ga), device_id_type=MESH).wait_send()
        if edge_steps and reach == 1:
            all_ = (pl.ds(0, edge_steps), pl.ds(edge_at[slot], edge))
            pltpu.make_async_remote_copy(
                edge_relay.at[all_], edge_near.at[(slot, *all_)], forward_send.at[1], edge_recv.at[slot, 0],
                device_id=(me, ga), device_id_type=MESH).wait_send()

    for p in range(planes if relays else 0):
        for slot, mid, most in ((0, up_mid, planes - 1 - p), (1, down_mid, p)):
            @pl.when(mid & (last == p))
            def _(slot=slot, most=most):
                forwarded(slot, *(sum(c % planes < most for c in range(m)) for m in (CHUNKS, EDGES)))
    for step_ in range(1, n_ga):
        tile_copy(step_).wait_send()


def plane_size(mesh):
    axis = mesh.axis_names.index("band")
    line = mesh.devices.take(0, axis=1 - axis)
    coords = [getattr(d, "coords", None) for d in line]
    if coords[0] is None:
        return len(coords)
    return sum(c[2] == coords[0][2] for c in coords)


def solution(mesh):
    n, n_ga = mesh.shape["band"], mesh.shape["ga"]
    plane = plane_size(mesh)

    def rotate(level, psi, tiles, half_width):
        rows, width = psi.shape
        span = tiles.shape[1]
        sides = span - 1
        edge = LANES * (level + 1) // LEVELS
        f32, bf16 = jnp.float32, jnp.bfloat16
        dma = pltpu.SemaphoreType.DMA
        edge_shape = (EDGES, LANES, rows // EDGES)
        return pl.pallas_call(
            functools.partial(kernel, n, n_ga, plane, edge),
            out_shape=pltpu.VMEM((rows, width), f32),
            in_specs=[
                pl.BlockSpec(memory_space=pl.ANY),
                pl.BlockSpec(memory_space=pl.ANY),
                pl.BlockSpec(memory_space=pl.ANY),
            ],
            out_specs=pl.BlockSpec(memory_space=pltpu.VMEM),
            scratch_shapes=[
                pltpu.SMEM((1,), jnp.int32),
                pltpu.VMEM((span, rows, width), f32),
                pltpu.VMEM((rows, width), f32),
                pltpu.VMEM((span, width, width), f32),
                pltpu.VMEM((span, width, width), bf16),
                pltpu.VMEM((span, width, width), bf16),
                pltpu.VMEM((2, *edge_shape), f32),
                pltpu.VMEM((2, *edge_shape), f32),
                pltpu.VMEM(edge_shape, f32),
                dma((3,)),
                dma((n_ga - 1,)),
                dma((n_ga - 1,)),
                dma((sides,)),
                dma((sides, CHUNKS)),
                dma((CHUNKS,)),
                dma((2,)),
                dma((2,)),
                dma((2, EDGES)),
                dma((EDGES,)),
            ],
            compiler_params=pltpu.CompilerParams(
                collective_id=level, has_side_effects=True, vmem_limit_bytes=52 * 2**20),
            name=f"rotate_{edge}",
        )(half_width, psi, tiles)

    def on_device(psi, tiles, half_width):
        width = psi.shape[1]
        reach = (tiles.shape[1] - 1) // 2
        beyond = half_width[0] - (reach * width - LANES + 1)
        level = lax.shift_right_arithmetic(beyond, (LANES // LEVELS).bit_length() - 1)
        branches = [functools.partial(rotate, i) for i in range(LEVELS)]
        return lax.switch(level, branches, psi, tiles, half_width)

    return jax.shard_map(
        on_device,
        mesh=mesh,
        in_specs=(P("ga", "band"), P("band", None, "ga", None), P()),
        out_specs=P("ga", "band"),
        check_vma=False,
    )
```

```python
import functools

import jax
import jax.numpy as jnp
from jax import lax
from jax.experimental import pallas as pl
from jax.experimental.pallas import tpu as pltpu
from jax.sharding import PartitionSpec as P

MESH = pl.DeviceIdType.MESH
CHUNKS = 8
FIRST = 2
EDGES = 4
PIECES = 2
LANES = 128
LEVELS = 16
AHEAD = 2


def split(x):
    high = x.astype(jnp.bfloat16)
    return high, (x - high.astype(jnp.float32)).astype(jnp.bfloat16)


def product(x, high, low):
    x_high, x_low = split(x)
    dot = functools.partial(jnp.dot, preferred_element_type=jnp.float32)
    return dot(x_high, high) + (dot(x_high, low) + dot(x_low, high))


def kernel(n, n_ga, plane, edge, half_width, psi, tiles, out, held, near, relay, raw, high, low,
           edge_own, edge_near, edge_relay, own_sem, tile_send, tile_recv, send, recv, relay_recv,
           forward_send, edge_send, edge_recv, edge_relay_recv):
    me = lax.axis_index("band")
    ga = lax.axis_index("ga")
    rows, width = psi.shape
    span, part = tiles.shape[1], tiles.shape[2]
    reach = (span - 1) // 2
    chunk = rows // CHUNKS
    sides = span - 1
    group = CHUNKS // EDGES
    edge_at = (LANES - edge, 0)
    planes = n // plane
    relays = plane >= 4 and planes > 1
    moves = [s * m for m in range(1, reach + 1) for s in (1, -1)]
    pieces_ = 1 if relays and CHUNKS % planes else PIECES
    at, last = lax.rem(me, plane), lax.div(me, plane)

    peers = []
    for move in moves:
        there = me + move
        peers.append(((there >= 0) & (there < n), there))
    up_src = (at == plane - 1) & (last < planes - 1)
    up_mid = (at == 0) & (last < planes - 1)
    up_dst = (at == 0) & (last > 0)
    down_src = (at == 0) & (last > 0)
    down_mid = (at == plane - 1) & (last > 0)
    down_dst = (at == plane - 1) & (last < planes - 1)
    up_mid_of_src = me - (plane - 1)
    down_mid_of_src = me + (plane - 1)
    if relays:
        peers += [
            (up_src, me - (plane - 1)), (up_mid, me + (plane - 1)),
            (up_mid, me + plane), (up_dst, me - plane),
            (down_src, me + (plane - 1)), (down_mid, me - (plane - 1)),
            (down_mid, me - plane), (down_dst, me + plane),
        ]
    barrier = pltpu.get_barrier_semaphore()
    count = jnp.int32(n_ga - 1)
    for step in range(1, n_ga):
        pl.semaphore_signal(barrier, inc=1, device_id=(me, lax.rem(ga + step, n_ga)), device_id_type=MESH)
    for cond, peer in peers:
        @pl.when(cond)
        def _(peer=peer):
            pl.semaphore_signal(barrier, inc=1, device_id=(peer, ga), device_id_type=MESH)
        count = count + cond.astype(jnp.int32)
    pl.semaphore_wait(barrier, count)

    def block(c):
        return pl.ds(pl.multiple_of(c * chunk, chunk), chunk)

    def columns(slot, move):
        if abs(move) != reach:
            return pl.ds(0, width)
        return pl.ds(LANES if slot % 2 == 0 else 0, width - LANES)

    def direct_copy(slot, move, c):
        at_ = (block(c), columns(slot, move))
        return pltpu.make_async_remote_copy(
            psi.at[at_], near.at[(slot, *at_)], send.at[slot], recv.at[slot, c],
            device_id=(me + move, ga), device_id_type=MESH)

    def piece_of(i):
        return pl.ds(pl.multiple_of((CHUNKS - 1) * chunk + i * (chunk // pieces_), chunk // pieces_), chunk // pieces_)

    def piece_copy(slot, move, i):
        at_ = (piece_of(i), columns(slot, move))
        return pltpu.make_async_remote_copy(
            psi.at[at_], near.at[(slot, *at_)], send.at[slot], recv.at[slot, CHUNKS - 1 + i],
            device_id=(me + move, ga), device_id_type=MESH)

    def relay_copy(slot, mid, c):
        at_ = (block(c), columns(slot, moves[slot]))
        return pltpu.make_async_remote_copy(
            psi.at[at_], relay.at[at_], send.at[slot], relay_recv.at[c],
            device_id=(mid, ga), device_id_type=MESH)

    def forward_copy(slot, to, c):
        at_ = (block(c), columns(slot, moves[slot]))
        return pltpu.make_async_remote_copy(
            relay.at[at_], near.at[(slot, *at_)], forward_send.at[0], recv.at[slot, c],
            device_id=(to, ga), device_id_type=MESH)

    def edge_direct(side, move, c):
        at_ = pl.ds(edge_at[side], edge)
        return pltpu.make_async_remote_copy(
            edge_own.at[side, c, at_], edge_near.at[side, c, at_],
            edge_send.at[side], edge_recv.at[side, c],
            device_id=(me + move, ga), device_id_type=MESH)

    def edge_relayed(side, mid, c):
        at_ = pl.ds(edge_at[side], edge)
        return pltpu.make_async_remote_copy(
            edge_own.at[side, c, at_], edge_relay.at[c, at_],
            edge_send.at[side], edge_relay_recv.at[c],
            device_id=(mid, ga), device_id_type=MESH)

    def edge_forward(side, to, c):
        at_ = pl.ds(edge_at[side], edge)
        return pltpu.make_async_remote_copy(
            edge_relay.at[c, at_], edge_near.at[side, c, at_],
            forward_send.at[1], edge_recv.at[side, c],
            device_id=(to, ga), device_id_type=MESH)

    def goes_up(p, c):
        return lax.rem(c, planes) < planes - 1 - p

    def goes_down(p, c):
        return lax.rem(c, planes) < p

    def tile_copy(step):
        peer = lax.rem(ga + step, n_ga)
        return pltpu.make_async_remote_copy(
            tiles.at[0], raw.at[:, pl.ds(pl.multiple_of(ga * part, part), part), :],
            tile_send.at[step - 1], tile_recv.at[step - 1],
            device_id=(me, peer), device_id_type=MESH)

    def send_from(slot, move, c, straight, through):
        there = me + move
        valid = (there >= 0) & (there < n)
        if relays and abs(move) == 1:
            src, mid = (up_src, up_mid_of_src) if move == 1 else (down_src, down_mid_of_src)
            via = src & (goes_up(last, c) if move == 1 else goes_down(last, c))

            @pl.when(via)
            def _():
                through(slot, mid, c).start()
            valid = valid & jnp.logical_not(via)

        @pl.when(valid)
        def _():
            straight(slot, move, c).start()

    def start(c, carry):
        for slot, move in enumerate(moves):
            send_from(slot, move, c, direct_copy, relay_copy)
        return carry

    lax.fori_loop(0, FIRST, start, 0)
    for step in range(1, n_ga):
        tile_copy(step).start()

    own = near.at[sides]
    own_psi = pltpu.make_async_copy(psi, own, own_sem.at[0])
    own_psi.start()
    own_tiles = pltpu.make_async_copy(
        tiles.at[0], raw.at[:, pl.ds(pl.multiple_of(ga * part, part), part), :], own_sem.at[1])
    own_tiles.start()
    own_half = pltpu.make_async_copy(half_width, held, own_sem.at[2])
    own_half.start()
    own_psi.wait()
    outer = (reach, -reach)

    def lanes_of(c):
        return pl.ds(pl.multiple_of(lax.rem(c, group) * chunk, chunk), chunk)

    def turn_edge(c, carry):
        g = lax.div(c, group)
        edge_own[0, g, :, lanes_of(c)] = jnp.transpose(own[block(c), 0:LANES])
        edge_own[1, g, :, lanes_of(c)] = jnp.transpose(own[block(c), width - LANES:width])

        @pl.when(lax.rem(c, group) == group - 1)
        def _():
            for side, move in enumerate(outer):
                send_from(side, move, g, edge_direct, edge_relayed)
        return carry
    lax.fori_loop(0, CHUNKS, turn_edge, 0)
    lax.fori_loop(FIRST, CHUNKS - (pieces_ > 1), start, 0)
    if pieces_ > 1:
        for slot, move in enumerate(moves):
            @pl.when((me + move >= 0) & (me + move < n))
            def _(slot=slot, move=move):
                for i in range(pieces_):
                    piece_copy(slot, move, i).start()

    def clear(c, carry):
        out[block(c), :] = jnp.zeros((chunk, width), jnp.float32)
        if edge < LANES:
            blank = jnp.zeros((LANES - edge, chunk), jnp.float32)
            g = lax.div(c, group)
            edge_near[0, g, 0:LANES - edge, lanes_of(c)] = blank
            edge_near[1, g, edge:LANES, lanes_of(c)] = blank
        return carry
    lax.fori_loop(0, CHUNKS, clear, 0)

    own_tiles.wait()
    for step in range(1, n_ga):
        tile_copy(step).wait_recv()
    own_half.wait()
    half = held[0]
    piece = min(width, 128)
    pieces = width // piece

    def mask(i, carry):
        k, r = lax.div(i, pieces), lax.rem(i, pieces) * piece
        at_ = pl.ds(pl.multiple_of(r, piece), piece)
        row = lax.broadcasted_iota(jnp.int32, (piece, width), 0) + (r + (k - reach) * width)
        col = lax.broadcasted_iota(jnp.int32, (piece, width), 1)
        u = jnp.where(jnp.abs(row - col) <= half, raw[k, at_, :], 0.0)
        high[k, at_, :], low[k, at_, :] = split(u)
        return carry
    lax.fori_loop(0, span * pieces, mask, 0)

    def pass_on(c, arrive, forward):
        @pl.when(up_mid & goes_up(last, c))
        def _():
            arrive(0, me, c).wait_recv()
            forward(0, me + plane, c).start()

        @pl.when(down_mid & goes_down(last, c))
        def _():
            arrive(1, me, c).wait_recv()
            forward(1, me - plane, c).start()

    def relay_on(c):
        pass_on(c, relay_copy, forward_copy)
        if reach == 1:
            g = c - (FIRST - 1)

            @pl.when((g >= 0) & (g < EDGES))
            def _():
                pass_on(g, edge_relayed, edge_forward)

    def arrived(slot, move, c, last_chunk=False):
        if abs(move) == reach:
            side = slot % 2
            g = lax.div(c, group)

            @pl.when(lax.rem(c, group) == 0)
            def _():
                edge_direct(side, move, g).wait_recv()
            lanes = slice(0, LANES) if side == 0 else slice(width - LANES, width)
            near[slot, block(c), lanes] = jnp.transpose(edge_near[side, g, :, lanes_of(c)])
        if pieces_ == 1:
            direct_copy(slot, move, c).wait_recv()
        elif not last_chunk:
            @pl.when(c < CHUNKS - 1)
            def _():
                direct_copy(slot, move, c).wait_recv()

            @pl.when(c == CHUNKS - 1)
            def _():
                for i in range(pieces_):
                    piece_copy(slot, move, i).wait_recv()

    in_chip = 1 - lax.rem(me, 2)

    def step(i, carry):
        turn, c = lax.div(i, CHUNKS), lax.rem(i, CHUNKS)
        if relays:
            ahead = i - (2 * CHUNKS - AHEAD)

            @pl.when((ahead >= 0) & (ahead < CHUNKS))
            def _():
                relay_on(ahead)

        def add(j, inner):
            other = j + (j >= in_chip).astype(jnp.int32)
            source = jnp.where(turn == 0, sides, jnp.where(turn == 1, in_chip, other))
            far = lax.div(source, 2) + 1
            move = jnp.where(turn == 0, 0, jnp.where(lax.rem(source, 2) == 0, far, -far))
            back = me - move

            @pl.when((back >= 0) & (back < n))
            def _():
                for slot, move_ in enumerate(moves):
                    @pl.when(source == slot)
                    def _(slot=slot, move_=move_):
                        arrived(slot, move_, c)
                k = reach - move
                out[block(c), :] += product(near[source, block(c), :], high[k], low[k])
            return inner
        return lax.fori_loop(0, jnp.where(turn == 2, sides - 1, 1), add, carry)
    lax.fori_loop(0, 3 * CHUNKS - (pieces_ > 1), step, 0)
    for slot, move in enumerate(moves if pieces_ > 1 else ()):
        @pl.when((me - move >= 0) & (me - move < n) & (in_chip != slot))
        def _(slot=slot, move=move):
            arrived(slot, move, jnp.int32(CHUNKS - 1), True)

            def add_piece(i, inner):
                piece_copy(slot, move, i).wait_recv()
                k = reach - move
                out[piece_of(i), :] += product(near[slot, piece_of(i), :], high[k], low[k])
                return inner
            lax.fori_loop(0, pieces_, add_piece, 0)

    for slot, move in enumerate(moves):
        there = me + move

        @pl.when((there >= 0) & (there < n))
        def _(slot=slot, move=move):
            all_ = (pl.ds(0, rows), columns(slot, move))
            pltpu.make_async_remote_copy(
                psi.at[all_], near.at[(slot, *all_)], send.at[slot], recv.at[slot, 0],
                device_id=(me + move, ga), device_id_type=MESH).wait_send()
            if abs(move) == reach:
                side = slot % 2
                all_ = (side, pl.ds(0, EDGES), pl.ds(edge_at[side], edge))
                pltpu.make_async_remote_copy(
                    edge_own.at[all_], edge_near.at[all_], edge_send.at[side], edge_recv.at[side, 0],
                    device_id=(me + move, ga), device_id_type=MESH).wait_send()

    def forwarded(slot, steps, edge_steps):
        if steps:
            all_ = (pl.ds(0, steps * chunk), columns(slot, moves[slot]))
            pltpu.make_async_remote_copy(
                relay.at[all_], near.at[(slot, *all_)], forward_send.at[0], recv.at[slot, 0],
                device_id=(me, ga), device_id_type=MESH).wait_send()
        if edge_steps and reach == 1:
            all_ = (pl.ds(0, edge_steps), pl.ds(edge_at[slot], edge))
            pltpu.make_async_remote_copy(
                edge_relay.at[all_], edge_near.at[(slot, *all_)], forward_send.at[1], edge_recv.at[slot, 0],
                device_id=(me, ga), device_id_type=MESH).wait_send()

    for p in range(planes if relays else 0):
        for slot, mid, most in ((0, up_mid, planes - 1 - p), (1, down_mid, p)):
            @pl.when(mid & (last == p))
            def _(slot=slot, most=most):
                forwarded(slot, *(sum(c % planes < most for c in range(m)) for m in (CHUNKS, EDGES)))
    for step_ in range(1, n_ga):
        tile_copy(step_).wait_send()


def plane_size(mesh):
    axis = mesh.axis_names.index("band")
    line = mesh.devices.take(0, axis=1 - axis)
    coords = [getattr(d, "coords", None) for d in line]
    if coords[0] is None:
        return len(coords)
    return sum(c[2] == coords[0][2] for c in coords)


def solution(mesh):
    n, n_ga = mesh.shape["band"], mesh.shape["ga"]
    plane = plane_size(mesh)

    def rotate(level, psi, tiles, half_width):
        rows, width = psi.shape
        span = tiles.shape[1]
        sides = span - 1
        edge = LANES * (level + 1) // LEVELS
        f32, bf16 = jnp.float32, jnp.bfloat16
        dma = pltpu.SemaphoreType.DMA
        edge_shape = (EDGES, LANES, rows // EDGES)
        return pl.pallas_call(
            functools.partial(kernel, n, n_ga, plane, edge),
            out_shape=pltpu.VMEM((rows, width), f32),
            in_specs=[
                pl.BlockSpec(memory_space=pl.ANY),
                pl.BlockSpec(memory_space=pl.ANY),
                pl.BlockSpec(memory_space=pl.ANY),
            ],
            out_specs=pl.BlockSpec(memory_space=pltpu.VMEM),
            scratch_shapes=[
                pltpu.SMEM((1,), jnp.int32),
                pltpu.VMEM((span, rows, width), f32),
                pltpu.VMEM((rows, width), f32),
                pltpu.VMEM((span, width, width), f32),
                pltpu.VMEM((span, width, width), bf16),
                pltpu.VMEM((span, width, width), bf16),
                pltpu.VMEM((2, *edge_shape), f32),
                pltpu.VMEM((2, *edge_shape), f32),
                pltpu.VMEM(edge_shape, f32),
                dma((3,)),
                dma((n_ga - 1,)),
                dma((n_ga - 1,)),
                dma((sides,)),
                dma((sides, CHUNKS + PIECES - 1)),
                dma((CHUNKS,)),
                dma((2,)),
                dma((2,)),
                dma((2, EDGES)),
                dma((EDGES,)),
            ],
            compiler_params=pltpu.CompilerParams(
                collective_id=level, has_side_effects=True, vmem_limit_bytes=52 * 2**20),
            name=f"rotate_{edge}",
        )(half_width, psi, tiles)

    def on_device(psi, tiles, half_width):
        width = psi.shape[1]
        reach = (tiles.shape[1] - 1) // 2
        beyond = half_width[0] - (reach * width - LANES + 1)
        level = lax.shift_right_arithmetic(beyond, (LANES // LEVELS).bit_length() - 1)
        branches = [functools.partial(rotate, i) for i in range(LEVELS)]
        return lax.switch(level, branches, psi, tiles, half_width)

    return jax.shard_map(
        on_device,
        mesh=mesh,
        in_specs=(P("ga", "band"), P("band", None, "ga", None), P()),
        out_specs=P("ga", "band"),
        check_vma=False,
    )
```

```python
import functools

import jax
import jax.numpy as jnp
from jax import lax
from jax.experimental import pallas as pl
from jax.experimental.pallas import tpu as pltpu
from jax.sharding import PartitionSpec as P

MESH = pl.DeviceIdType.MESH
CHUNKS = 8
FIRST = 2
EDGES = 4
LANES = 128
LEVELS = 16
AHEAD = 2


def split(x):
    high = x.astype(jnp.bfloat16)
    return high, (x - high.astype(jnp.float32)).astype(jnp.bfloat16)


def product(x, high, low):
    x_high, x_low = split(x)
    dot = functools.partial(jnp.dot, preferred_element_type=jnp.float32)
    return dot(x_high, high) + (dot(x_high, low) + dot(x_low, high))


def kernel(n, n_ga, plane, edge, half_width, psi, tiles, out, held, near, relay, raw, high, low,
           edge_own, edge_near, edge_relay, own_sem, tile_send, tile_recv, send, recv, relay_recv,
           forward_send, edge_send, edge_recv, edge_relay_recv):
    me = lax.axis_index("band")
    ga = lax.axis_index("ga")
    rows, width = psi.shape
    span, part = tiles.shape[1], tiles.shape[2]
    reach = (span - 1) // 2
    chunk = rows // CHUNKS
    sides = span - 1
    group = CHUNKS // EDGES
    edge_at = (LANES - edge, 0)
    planes = n // plane
    relays = plane >= 4 and planes > 1
    moves = [s * m for m in range(1, reach + 1) for s in (1, -1)]
    at, last = lax.rem(me, plane), lax.div(me, plane)

    peers = []
    for move in moves:
        there = me + move
        peers.append(((there >= 0) & (there < n), there))
    up_src = (at == plane - 1) & (last < planes - 1)
    up_mid = (at == 0) & (last < planes - 1)
    up_dst = (at == 0) & (last > 0)
    down_src = (at == 0) & (last > 0)
    down_mid = (at == plane - 1) & (last > 0)
    down_dst = (at == plane - 1) & (last < planes - 1)
    up_mid_of_src = me - (plane - 1)
    down_mid_of_src = me + (plane - 1)
    if relays:
        peers += [
            (up_src, me - (plane - 1)), (up_mid, me + (plane - 1)),
            (up_mid, me + plane), (up_dst, me - plane),
            (down_src, me + (plane - 1)), (down_mid, me - (plane - 1)),
            (down_mid, me - plane), (down_dst, me + plane),
        ]
    barrier = pltpu.get_barrier_semaphore()
    count = jnp.int32(n_ga - 1)
    for step in range(1, n_ga):
        pl.semaphore_signal(barrier, inc=1, device_id=(me, lax.rem(ga + step, n_ga)), device_id_type=MESH)
    for cond, peer in peers:
        @pl.when(cond)
        def _(peer=peer):
            pl.semaphore_signal(barrier, inc=1, device_id=(peer, ga), device_id_type=MESH)
        count = count + cond.astype(jnp.int32)
    pl.semaphore_wait(barrier, count)

    def block(c):
        return pl.ds(pl.multiple_of(c * chunk, chunk), chunk)

    def columns(slot, move):
        if abs(move) != reach:
            return pl.ds(0, width)
        return pl.ds(LANES if slot % 2 == 0 else 0, width - LANES)

    def direct_copy(slot, move, c):
        at_ = (block(c), columns(slot, move))
        return pltpu.make_async_remote_copy(
            psi.at[at_], near.at[(slot, *at_)], send.at[slot], recv.at[slot, c],
            device_id=(me + move, ga), device_id_type=MESH)

    def relay_copy(slot, mid, c):
        at_ = (block(c), columns(slot, moves[slot]))
        return pltpu.make_async_remote_copy(
            psi.at[at_], relay.at[at_], send.at[slot], relay_recv.at[c],
            device_id=(mid, ga), device_id_type=MESH)

    def forward_copy(slot, to, c):
        at_ = (block(c), columns(slot, moves[slot]))
        return pltpu.make_async_remote_copy(
            relay.at[at_], near.at[(slot, *at_)], forward_send.at[0], recv.at[slot, c],
            device_id=(to, ga), device_id_type=MESH)

    def edge_direct(side, move, c):
        at_ = pl.ds(edge_at[side], edge)
        return pltpu.make_async_remote_copy(
            edge_own.at[side, c, at_], edge_near.at[side, c, at_],
            edge_send.at[side], edge_recv.at[side, c],
            device_id=(me + move, ga), device_id_type=MESH)

    def edge_relayed(side, mid, c):
        at_ = pl.ds(edge_at[side], edge)
        return pltpu.make_async_remote_copy(
            edge_own.at[side, c, at_], edge_relay.at[c, at_],
            edge_send.at[side], edge_relay_recv.at[c],
            device_id=(mid, ga), device_id_type=MESH)

    def edge_forward(side, to, c):
        at_ = pl.ds(edge_at[side], edge)
        return pltpu.make_async_remote_copy(
            edge_relay.at[c, at_], edge_near.at[side, c, at_],
            forward_send.at[1], edge_recv.at[side, c],
            device_id=(to, ga), device_id_type=MESH)

    def goes_up(p, c):
        return lax.rem(c, planes) < planes - 1 - p

    def goes_down(p, c):
        return lax.rem(c, planes) < p

    def tile_copy(step):
        peer = lax.rem(ga + step, n_ga)
        return pltpu.make_async_remote_copy(
            tiles.at[0], raw.at[:, pl.ds(pl.multiple_of(ga * part, part), part), :],
            tile_send.at[step - 1], tile_recv.at[step - 1],
            device_id=(me, peer), device_id_type=MESH)

    def send_from(slot, move, c, straight, through):
        there = me + move
        valid = (there >= 0) & (there < n)
        if relays and abs(move) == 1:
            src, mid = (up_src, up_mid_of_src) if move == 1 else (down_src, down_mid_of_src)
            via = src & (goes_up(last, c) if move == 1 else goes_down(last, c))

            @pl.when(via)
            def _():
                through(slot, mid, c).start()
            valid = valid & jnp.logical_not(via)

        @pl.when(valid)
        def _():
            straight(slot, move, c).start()

    def start(c, carry):
        for slot, move in enumerate(moves):
            send_from(slot, move, c, direct_copy, relay_copy)
        return carry

    lax.fori_loop(0, FIRST, start, 0)
    for step in range(1, n_ga):
        tile_copy(step).start()

    own = near.at[sides]
    own_psi = pltpu.make_async_copy(psi, own, own_sem.at[0])
    own_psi.start()
    own_tiles = pltpu.make_async_copy(
        tiles.at[0], raw.at[:, pl.ds(pl.multiple_of(ga * part, part), part), :], own_sem.at[1])
    own_tiles.start()
    own_half = pltpu.make_async_copy(half_width, held, own_sem.at[2])
    own_half.start()
    own_psi.wait()
    outer = (reach, -reach)

    def lanes_of(c):
        return pl.ds(pl.multiple_of(lax.rem(c, group) * chunk, chunk), chunk)

    def turn_edge(c, carry):
        g = lax.div(c, group)
        edge_own[0, g, :, lanes_of(c)] = jnp.transpose(own[block(c), 0:LANES])
        edge_own[1, g, :, lanes_of(c)] = jnp.transpose(own[block(c), width - LANES:width])

        @pl.when(lax.rem(c, group) == group - 1)
        def _():
            for side, move in enumerate(outer):
                send_from(side, move, g, edge_direct, edge_relayed)
        return carry
    lax.fori_loop(0, CHUNKS, turn_edge, 0)
    lax.fori_loop(FIRST, CHUNKS, start, 0)

    def clear(c, carry):
        out[block(c), :] = jnp.zeros((chunk, width), jnp.float32)
        if edge < LANES:
            blank = jnp.zeros((LANES - edge, chunk), jnp.float32)
            g = lax.div(c, group)
            edge_near[0, g, 0:LANES - edge, lanes_of(c)] = blank
            edge_near[1, g, edge:LANES, lanes_of(c)] = blank
        return carry
    lax.fori_loop(0, CHUNKS, clear, 0)

    own_tiles.wait()
    for step in range(1, n_ga):
        tile_copy(step).wait_recv()
    own_half.wait()
    half = held[0]
    piece = min(width, 128)
    pieces = width // piece

    def mask(i, carry):
        k, r = lax.div(i, pieces), lax.rem(i, pieces) * piece
        at_ = pl.ds(pl.multiple_of(r, piece), piece)
        row = lax.broadcasted_iota(jnp.int32, (piece, width), 0) + (r + (k - reach) * width)
        col = lax.broadcasted_iota(jnp.int32, (piece, width), 1)
        u = jnp.where(jnp.abs(row - col) <= half, raw[k, at_, :], 0.0)
        high[k, at_, :], low[k, at_, :] = split(u)
        return carry
    lax.fori_loop(0, span * pieces, mask, 0)

    def pass_on(c, arrive, forward):
        @pl.when(up_mid & goes_up(last, c))
        def _():
            arrive(0, me, c).wait_recv()
            forward(0, me + plane, c).start()

        @pl.when(down_mid & goes_down(last, c))
        def _():
            arrive(1, me, c).wait_recv()
            forward(1, me - plane, c).start()

    def relay_on(c):
        pass_on(c, relay_copy, forward_copy)
        if reach == 1:
            g = c - (FIRST - 1)

            @pl.when((g >= 0) & (g < EDGES))
            def _():
                pass_on(g, edge_relayed, edge_forward)

    def arrived(slot, move, c):
        if abs(move) == reach:
            side = slot % 2
            g = lax.div(c, group)

            @pl.when(lax.rem(c, group) == 0)
            def _():
                edge_direct(side, move, g).wait_recv()
            lanes = slice(0, LANES) if side == 0 else slice(width - LANES, width)
            near[slot, block(c), lanes] = jnp.transpose(edge_near[side, g, :, lanes_of(c)])
        direct_copy(slot, move, c).wait_recv()

    in_chip = 1 - lax.rem(me, 2)

    def step(i, carry):
        turn, c = lax.div(i, CHUNKS), lax.rem(i, CHUNKS)
        if relays:
            ahead = i - (2 * CHUNKS - AHEAD)

            @pl.when((ahead >= 0) & (ahead < CHUNKS))
            def _():
                relay_on(ahead)

        def add(j, inner):
            other = j + (j >= in_chip).astype(jnp.int32)
            source = jnp.where(turn == 0, sides, jnp.where(turn == 1, in_chip, other))
            far = lax.div(source, 2) + 1
            move = jnp.where(turn == 0, 0, jnp.where(lax.rem(source, 2) == 0, far, -far))
            back = me - move

            @pl.when((back >= 0) & (back < n))
            def _():
                for slot, move_ in enumerate(moves):
                    @pl.when(source == slot)
                    def _(slot=slot, move_=move_):
                        arrived(slot, move_, c)
                k = reach - move
                out[block(c), :] += product(near[source, block(c), :], high[k], low[k])
            return inner
        return lax.fori_loop(0, jnp.where(turn == 2, sides - 1, 1), add, carry)
    lax.fori_loop(0, 3 * CHUNKS, step, 0)

    for slot, move in enumerate(moves):
        there = me + move

        @pl.when((there >= 0) & (there < n))
        def _(slot=slot, move=move):
            all_ = (pl.ds(0, rows), columns(slot, move))
            pltpu.make_async_remote_copy(
                psi.at[all_], near.at[(slot, *all_)], send.at[slot], recv.at[slot, 0],
                device_id=(me + move, ga), device_id_type=MESH).wait_send()
            if abs(move) == reach:
                side = slot % 2
                all_ = (side, pl.ds(0, EDGES), pl.ds(edge_at[side], edge))
                pltpu.make_async_remote_copy(
                    edge_own.at[all_], edge_near.at[all_], edge_send.at[side], edge_recv.at[side, 0],
                    device_id=(me + move, ga), device_id_type=MESH).wait_send()

    def forwarded(slot, steps, edge_steps):
        if steps:
            all_ = (pl.ds(0, steps * chunk), columns(slot, moves[slot]))
            pltpu.make_async_remote_copy(
                relay.at[all_], near.at[(slot, *all_)], forward_send.at[0], recv.at[slot, 0],
                device_id=(me, ga), device_id_type=MESH).wait_send()
        if edge_steps and reach == 1:
            all_ = (pl.ds(0, edge_steps), pl.ds(edge_at[slot], edge))
            pltpu.make_async_remote_copy(
                edge_relay.at[all_], edge_near.at[(slot, *all_)], forward_send.at[1], edge_recv.at[slot, 0],
                device_id=(me, ga), device_id_type=MESH).wait_send()

    for p in range(planes if relays else 0):
        for slot, mid, most in ((0, up_mid, planes - 1 - p), (1, down_mid, p)):
            @pl.when(mid & (last == p))
            def _(slot=slot, most=most):
                forwarded(slot, *(sum(c % planes < most for c in range(m)) for m in (CHUNKS, EDGES)))
    for step_ in range(1, n_ga):
        tile_copy(step_).wait_send()


def plane_size(mesh):
    axis = mesh.axis_names.index("band")
    line = mesh.devices.take(0, axis=1 - axis)
    coords = [getattr(d, "coords", None) for d in line]
    if coords[0] is None:
        return len(coords)
    return sum(c[2] == coords[0][2] for c in coords)


def solution(mesh):
    n, n_ga = mesh.shape["band"], mesh.shape["ga"]
    plane = plane_size(mesh)

    def rotate(level, psi, tiles, half_width):
        rows, width = psi.shape
        span = tiles.shape[1]
        sides = span - 1
        edge = LANES * (level + 1) // LEVELS
        f32, bf16 = jnp.float32, jnp.bfloat16
        dma = pltpu.SemaphoreType.DMA
        edge_shape = (EDGES, LANES, rows // EDGES)
        return pl.pallas_call(
            functools.partial(kernel, n, n_ga, plane, edge),
            out_shape=pltpu.VMEM((rows, width), f32),
            in_specs=[
                pl.BlockSpec(memory_space=pl.ANY),
                pl.BlockSpec(memory_space=pl.ANY),
                pl.BlockSpec(memory_space=pl.ANY),
            ],
            out_specs=pl.BlockSpec(memory_space=pltpu.VMEM),
            scratch_shapes=[
                pltpu.SMEM((1,), jnp.int32),
                pltpu.VMEM((span, rows, width), f32),
                pltpu.VMEM((rows, width), f32),
                pltpu.VMEM((span, width, width), f32),
                pltpu.VMEM((span, width, width), bf16),
                pltpu.VMEM((span, width, width), bf16),
                pltpu.VMEM((2, *edge_shape), f32),
                pltpu.VMEM((2, *edge_shape), f32),
                pltpu.VMEM(edge_shape, f32),
                dma((3,)),
                dma((n_ga - 1,)),
                dma((n_ga - 1,)),
                dma((sides,)),
                dma((sides, CHUNKS)),
                dma((CHUNKS,)),
                dma((2,)),
                dma((2,)),
                dma((2, EDGES)),
                dma((EDGES,)),
            ],
            compiler_params=pltpu.CompilerParams(
                collective_id=level, has_side_effects=True, vmem_limit_bytes=52 * 2**20),
            name=f"rotate_{edge}",
        )(half_width, psi, tiles)

    def on_device(psi, tiles, half_width):
        width = psi.shape[1]
        reach = (tiles.shape[1] - 1) // 2
        beyond = half_width[0] - (reach * width - LANES + 1)
        level = lax.shift_right_arithmetic(beyond, (LANES // LEVELS).bit_length() - 1)
        branches = [functools.partial(rotate, i) for i in range(LEVELS)]
        return lax.switch(level, branches, psi, tiles, half_width)

    return jax.shard_map(
        on_device,
        mesh=mesh,
        in_specs=(P("ga", "band"), P("band", None, "ga", None), P()),
        out_specs=P("ga", "band"),
        check_vma=False,
    )
```
